32 devices in a mesh: grp: 2 (over x), slab: 16 (over z, y, core).
Axes of the slice: x: 2, y: 2, z: 4, core: 2. Of those that a mesh axis runs over, the one named last changes fastest.
Arguments:
- estimate: float32 [2, 8, 4, 48, 32], P(None, None, 'grp', 'slab'), parts along dimension 2, may hold values from -6 to 6
- measured: float32 [2, 8, 4, 48, 32], P(None, None, 'grp', 'slab'), parts along dimension 2, may hold values from -6 to 6
- sampled_lines: int32 [4, 12], P('grp'), parts along dimension 0, may hold values from 0 to 47, as said below
Outputs:
- updated: float32 [2, 8, 4, 48, 32], P(None, None, 'grp', 'slab'), parts along dimension 2
The draws below stay inside these ranges and needn't reach their ends.
There are 2 independent parts, one for each index of `grp`. The reference program is written for one: setup_inputs(seed, part) draws one part's arguments, and reference() takes and returns one part's arrays. A program takes and returns all parts, laid end to end along the dimension named above; each array names one. Nothing has to cross between parts.
Inputs may be any that keep to these rules, and one draw needn't show every extreme that they name: `sampled_lines`: lines within a frame are distinct, and every frame contains line 48 // 2.
All inputs are finite; a program needn't handle non-finite values.
Results may differ from the reference program's by a relative error of at most 0.0001.
Values sent between devices are 32-bit elements; how exact they have to be, the bound alone decides.
A program may use at most 64 MiB of HBM per device.

```python
import jax
import jax.numpy as jnp
from jax import lax

C = 8
T_SIZE = 2
KXW = 32
KY_DEV = 3
KY = 48
NS = 12
N_SLAB = 16


def draw_sampled_lines(key, part):
    frames = jnp.arange(T_SIZE, dtype=jnp.int32)

    def one_frame(frame):
        order = jax.random.permutation(jax.random.fold_in(key, frame), KY).astype(jnp.int32)
        centre = KY // 2
        where = jnp.argmax(order == centre)
        order = order.at[where].set(order[0]).at[0].set(centre)
        return order[:NS]
    return jax.vmap(one_frame)(frames).astype(jnp.int32)


def block_scale(stream_key, dims, cuts, smallest, high):
    def one(dim, parts):
        heights = jax.random.uniform(jax.random.fold_in(jax.random.fold_in(stream_key, 6), dim), (parts,), jnp.float32, smallest / len(cuts), high / len(cuts))
        return jnp.repeat(jnp.exp(heights), dims[dim] // parts).reshape((-1,) + (1,) * (len(dims) - dim - 1))

    gain = one(*cuts[0])
    for cut in cuts[1:]:
        gain = gain * one(*cut)
    return gain


def gaussian(rng, dims, spread, reach, cuts=(), held_as=jnp.bfloat16):
    drawn = jax.random.normal(rng, dims, jnp.float32) * spread
    if len(cuts) > 0:
        drawn = block_scale(rng, dims, cuts, -0.22, 0.18) * drawn
    return jnp.clip(drawn, min=-reach, max=reach).astype(held_as)


def setup_inputs(seed: int = 0, part: int = 0) -> dict:
    streams_of = jax.random.split(jax.random.key(seed), 4)
    part_splits = jax.random.split(jax.random.fold_in(streams_of[3], part), 4)
    return {
        "estimate": gaussian(part_splits[0], (2, C, T_SIZE, KY, KXW), 1.0, 6.0, ((3, 16),), jnp.float32),
        "measured": gaussian(part_splits[1], (2, C, T_SIZE, KY, KXW), 1.0, 6.0, ((3, 16),), jnp.float32),
        "sampled_lines": draw_sampled_lines(jax.random.fold_in(jax.random.fold_in(streams_of[3], part), 71), part),
    }


HIGH = lax.Precision.HIGHEST


def build_rows(ext, rows):
    pieces = []
    for shift_t in range(5):
        for shift_y in range(5):
            for shift_x in range(5):
                pieces.append(ext[:, :, shift_t:shift_t + T_SIZE, shift_y:shift_y + rows, shift_x:shift_x + KXW])
    stacked = jnp.stack(pieces, axis=-1)
    stacked = jnp.transpose(stacked, (0, 2, 3, 4, 1, 5))
    return stacked.reshape(2, T_SIZE * rows * KXW, C * 125)


def fold_rows(filtered, rows):
    shaped = filtered.reshape(2, T_SIZE, rows, KXW, C, 125)
    shaped = jnp.transpose(shaped, (0, 4, 1, 2, 3, 5))
    result = jnp.zeros((2, C, T_SIZE + 4, rows + 4, KXW + 4), jnp.float32)
    offset = 0
    for shift_t in range(5):
        for shift_y in range(5):
            for shift_x in range(5):
                result = result.at[:, :, shift_t:shift_t + T_SIZE, shift_y:shift_y + rows, shift_x:shift_x + KXW].add(shaped[..., offset])
                offset += 1
    return result / 125.0


def reference(estimate, measured, sampled_lines):
    padded = jnp.pad(estimate, ((0, 0), (0, 0), (2, 2), (2, 2), (2, 2)))
    width = 125 * C
    starts = jnp.arange(N_SLAB, dtype=jnp.int32) * KY_DEV

    def gram_step(carry, start):
        ext = lax.dynamic_slice_in_dim(padded, start, KY_DEV + 4, 3)
        patch = build_rows(ext, KY_DEV)
        real_part, imag_part = patch[0], patch[1]
        real_gram = jnp.dot(real_part.T, real_part, precision=HIGH) + jnp.dot(imag_part.T, imag_part, precision=HIGH)
        imag_gram = jnp.dot(real_part.T, imag_part, precision=HIGH) - jnp.dot(imag_part.T, real_part, precision=HIGH)
        return (carry[0] + real_gram, carry[1] + imag_gram), None

    zeros = jnp.zeros((width, width), jnp.float32)
    (real_gram, imag_gram), unused = lax.scan(gram_step, (zeros, zeros), starts)
    scale = jnp.trace(real_gram) / width + 1e-6
    real_gram = real_gram / scale
    imag_gram = imag_gram / scale

    def fold_step(total, start):
        ext = lax.dynamic_slice_in_dim(padded, start, KY_DEV + 4, 3)
        patch = build_rows(ext, KY_DEV)
        real_part, imag_part = patch[0], patch[1]
        real_out = jnp.dot(real_part, real_gram, precision=HIGH) - jnp.dot(imag_part, imag_gram, precision=HIGH)
        imag_out = jnp.dot(real_part, imag_gram, precision=HIGH) + jnp.dot(imag_part, real_gram, precision=HIGH)
        piece = fold_rows(jnp.stack([real_out, imag_out]), KY_DEV)
        current = lax.dynamic_slice_in_dim(total, start, KY_DEV + 4, 3)
        total = lax.dynamic_update_slice_in_dim(total, current + piece, start, 3)
        return total, None

    total = jnp.zeros((2, C, T_SIZE + 4, KY + 4, KXW + 4), jnp.float32)
    total, unused = lax.scan(fold_step, total, starts)
    folded = total[:, :, 2:-2, 2:-2, 2:-2]
    rows = jnp.arange(KY, dtype=jnp.int32)
    hit = jnp.any(sampled_lines[:, :, None] == rows[None, None, :], axis=1)
    weight = hit.astype(jnp.float32)[None, None, :, :, None]
    return weight * measured + (1.0 - weight) * folded
```

```python
import jax
import jax.numpy as jnp
from jax import lax
from jax.sharding import PartitionSpec as P

HIGH = lax.Precision.HIGH


def counts(frames):
    table = {}
    for s in range(frames):
        for s2 in range(frames):
            for d in range(-frames + 1, frames):
                if 0 <= s + d < frames and 0 <= s2 + d < frames:
                    n = sum(
                        1
                        for t in range(frames)
                        if 0 <= t + d < frames and abs(s - t) <= 2 and abs(s2 - t) <= 2
                    )
                    if n:
                        table[s, s2, d] = n
    return table


def local(estimate, measured, sampled_lines):
    _, coils, frames, rows, readout = estimate.shape
    width = 125 * coils
    count = lax.axis_size("slab")
    total = count * rows
    place = lax.axis_index("slab")
    full = lax.all_gather(estimate, "slab", axis=3, tiled=True)
    stride = readout + 4
    channels = 2 * frames * coils
    grid = jnp.transpose(full, (2, 0, 1, 3, 4)).reshape(channels, total, readout)
    grid = jnp.pad(grid, ((0, 0), (4, 5), (2, 2)))

    def patches(lines, span_lines):
        flat = lines.reshape(channels, -1)
        span = span_lines * stride
        valid = (jnp.arange(span, dtype=jnp.int32) % stride < readout).astype(jnp.float32)
        pieces = [
            flat[:, b * stride + e : b * stride + e + span] for b in range(5) for e in range(5)
        ]
        return jnp.stack(pieces).reshape(25 * channels, span) * valid

    piece = max(k for k in range(1, min(total, 48) + 1) if total % k == 0)

    def gram_of(start):
        every = patches(lax.dynamic_slice_in_dim(grid, start + 2, piece + 5, 1), piece)
        return lax.dot_general(every, every, (((1,), (1,)), ((), ())), precision=HIGH)

    if piece == total:
        gram = gram_of(0)
    else:
        gram = lax.fori_loop(
            1, total // piece, lambda k, sofar: sofar + gram_of(k * piece), gram_of(0)
        )
    g = gram.reshape(25, frames, 2, coils, 25, frames, 2, coils)
    re = g[:, :, 0, :, :, :, 0, :] + g[:, :, 1, :, :, :, 1, :]
    im = g[:, :, 0, :, :, :, 1, :] - g[:, :, 1, :, :, :, 0, :]
    reach = jnp.array(
        [sum(1 for t in range(frames) if abs(s - t) <= 2) for s in range(frames)], jnp.float32
    )
    per_frame = jnp.einsum("osposp->s", re)
    scale = jnp.sum(per_frame * reach) / width + 1e-06
    table = counts(frames)

    def coupled(m):
        outer = []
        for s in range(frames):
            inner = []
            for s2 in range(frames):
                terms = [
                    n * m[:, s + d, :, :, s2 + d, :]
                    for (p, q, d), n in table.items()
                    if (p, q) == (s, s2)
                ]
                inner.append(sum(terms))
            outer.append(jnp.stack(inner, axis=3))
        return jnp.stack(outer, axis=1)

    re, im = coupled(re), coupled(im)
    top = jnp.stack([re, im], axis=5)
    bottom = jnp.stack([-im, re], axis=5)
    weights = jnp.stack([top, bottom], axis=2).reshape(25 * channels, 25 * channels)
    near = lax.dynamic_slice_in_dim(grid, place * rows, rows + 9, 1)
    mine = patches(near, rows + 4)
    line = jnp.arange((rows + 4) * stride, dtype=jnp.int32) // stride + place * rows - 2
    inside = ((line >= 0) & (line < total)).astype(jnp.float32)
    mine = mine * inside
    filtered = lax.dot_general(weights, mine, (((0,), (0,)), ((), ())), precision=HIGH)
    filtered = filtered.reshape(25, channels, rows + 4, stride)
    filtered = jnp.pad(filtered, ((0, 0), (0, 0), (0, 0), (4, 0)))
    folded = 0.0
    for b in range(5):
        for e in range(5):
            folded = folded + filtered[5 * b + e, :, 4 - b : 4 - b + rows, 6 - e : 6 - e + readout]
    folded = folded / (125.0 * scale)
    folded = jnp.transpose(folded.reshape(frames, 2, coils, rows, readout), (1, 2, 0, 3, 4))
    line_index = place * rows + jnp.arange(rows, dtype=jnp.int32)
    hit = jnp.any(sampled_lines[:, :, None] == line_index[None, None, :], axis=1)
    return jnp.where(hit[None, None, :, :, None], measured, folded)


def solution(mesh):
    placed = (
        P(None, None, "grp", "slab", None),
        P(None, None, "grp", "slab", None),
        P("grp", None),
    )
    return jax.shard_map(
        local,
        mesh=mesh,
        in_specs=placed,
        out_specs=P(None, None, "grp", "slab", None),
        check_vma=False,
    )
```

```python
import functools

import jax
import jax.numpy as jnp
from jax import lax
from jax.experimental import pallas as pl
from jax.experimental.pallas import tpu as pltpu
from jax.sharding import PartitionSpec as P

LANES = 128


def gather_kernel(n, x_ref, out_ref, send_sem, recv_sem, own_sem):
    me = lax.axis_index("slab")

    def greet(k, carry):
        pl.semaphore_signal(
            pltpu.get_barrier_semaphore(), inc=1, device_id={"slab": lax.rem(me + k, n)}
        )
        return carry

    lax.fori_loop(1, n, greet, 0)
    own = pltpu.make_async_copy(x_ref, out_ref.at[me], own_sem)
    own.start()
    pl.semaphore_wait(pltpu.get_barrier_semaphore(), n - 1)

    def copy(k, place):
        return pltpu.make_async_remote_copy(
            src_ref=x_ref,
            dst_ref=out_ref.at[place],
            send_sem=send_sem.at[k - 1],
            recv_sem=recv_sem.at[k - 1],
            device_id={"slab": lax.rem(me + k, n)},
        )

    def send(k, carry):
        copy(k, me).start()
        return carry

    def receive(k, carry):
        copy(k, lax.rem(me + n - k, n)).wait_recv()
        return carry

    def finish(k, carry):
        copy(k, me).wait_send()
        return carry

    lax.fori_loop(1, n, send, 0)
    own.wait()
    lax.fori_loop(1, n, receive, 0)
    lax.fori_loop(1, n, finish, 0)


def gathered(block, n):
    return pl.pallas_call(
        functools.partial(gather_kernel, n),
        out_shape=jax.ShapeDtypeStruct((n,) + block.shape, block.dtype),
        in_specs=[pl.BlockSpec(memory_space=pltpu.VMEM)],
        out_specs=pl.BlockSpec(memory_space=pltpu.VMEM),
        scratch_shapes=[
            pltpu.SemaphoreType.DMA((n - 1,)),
            pltpu.SemaphoreType.DMA((n - 1,)),
            pltpu.SemaphoreType.DMA,
        ],
        compiler_params=pltpu.CompilerParams(collective_id=0, has_side_effects=True),
    )(block)


def couplings(frames):
    table = {}
    for s in range(frames):
        for s2 in range(frames):
            for d in range(1 - frames, frames):
                if 0 <= s + d < frames and 0 <= s2 + d < frames:
                    n = sum(
                        1
                        for t in range(frames)
                        if 0 <= t + d < frames and abs(s - t) <= 2 and abs(s2 - t) <= 2
                    )
                    if n:
                        table[s, s2, d] = n
    return table


def halves(x):
    hi = x.astype(jnp.bfloat16)
    return hi, (x - hi.astype(jnp.float32)).astype(jnp.bfloat16)


def dot_nt(a, b):
    return lax.dot_general(a, b, (((1,), (1,)), ((), ())), preferred_element_type=jnp.float32)


def dot_nn(a, b):
    return lax.dot_general(a, b, (((1,), (0,)), ((), ())), preferred_element_type=jnp.float32)


def filter_kernel(n, chunk, frames, coils, rows, readout, all_ref, out_ref, *scratch):
    q_hi, q_lo, l_hi, l_lo, e_hi, e_lo, p_hi, p_lo, m_hi, m_lo, s_ref = scratch
    me = lax.axis_index("slab")
    stride = readout + 4
    channels = 2 * frames * coils
    size = 5 * channels
    total = n * rows

    def window(d, halo, lanes):
        lane = lax.broadcasted_iota(jnp.int32, (channels, lanes), 1)
        result = jnp.zeros((channels, lanes), jnp.float32)
        reach = -(-halo // rows)
        for k in range(-reach, reach + 1):
            other = d + k
            block = all_ref[jnp.clip(other, 0, n - 1)]
            inside = (other >= 0) & (other < n)
            block = jnp.where(inside, block, 0.0)
            wide = jnp.concatenate(
                [block, jnp.zeros((channels, lanes - LANES), jnp.float32)], axis=1
            )
            start = (halo + k * rows) * stride
            moved = pltpu.roll(wide, start % lanes, 1) if start % lanes else wide
            low, high = max(start, 0), min(start + rows * stride, (rows + 2 * halo) * stride)
            result = jnp.where((lane >= low) & (lane < high), moved, result)
        return result

    def shifted(ext, b, keep):
        lanes = ext.shape[1]
        moved = []
        for e in range(5):
            off = b * stride + e
            moved.append((pltpu.roll(ext, lanes - off, 1) if off else ext)[:, :keep])
        return jnp.concatenate(
            [
                moved[e][g * coils : (g + 1) * coils]
                for g in range(2 * frames)
                for e in range(5)
            ],
            axis=0,
        )

    lane = lax.broadcasted_iota(jnp.int32, (1, LANES), 1)
    valid = (lane % stride < readout) & (lane < rows * stride)

    def gram_chunk(first):
        def build(k, carry):
            ext = window(first + k, 2, 2 * LANES)
            at = pl.ds(pl.multiple_of(k * LANES, LANES), LANES)
            for b in range(5):
                hi, lo = halves(shifted(ext, b, LANES))
                q_hi[pl.ds(b * size, size), at] = hi
                q_lo[pl.ds(b * size, size), at] = lo
                if b == 0:
                    l_hi[:, at] = jnp.where(valid, hi, jnp.zeros_like(hi))
                    l_lo[:, at] = jnp.where(valid, lo, jnp.zeros_like(lo))
            return carry

        lax.fori_loop(0, chunk, build, 0)
        for b in range(5):
            at = pl.ds(b * size, size)
            s_ref[at, :] += (
                dot_nt(q_hi[at, :], l_hi[...])
                + dot_nt(q_hi[at, :], l_lo[...])
                + dot_nt(q_lo[at, :], l_hi[...])
            )

    s_ref[...] = jnp.zeros_like(s_ref)
    if n == chunk:
        gram_chunk(0)
    else:
        lax.fori_loop(0, n // chunk, lambda k, c: (gram_chunk(k * chunk), c)[1], 0)

    for place, d in enumerate((0, n - 1)):
        ext = window(d, 2, 2 * LANES)
        for j, b in enumerate((2, 3)):
            hi, lo = halves(shifted(ext, b, LANES))
            e_hi[place * 2 + j] = hi
            e_lo[place * 2 + j] = lo

    def line_gram(place, line, dy):
        pick = (lane >= line * stride) & (lane < line * stride + readout)
        hi = jnp.where(pick, e_hi[place * 2], 0)
        lo = jnp.where(pick, e_lo[place * 2], 0)
        right_hi, right_lo = e_hi[place * 2 + dy], e_lo[place * 2 + dy]
        return dot_nt(right_hi, hi) + dot_nt(right_hi, lo) + dot_nt(right_lo, hi)

    sums = [s_ref[pl.ds(b * size, size), :] for b in range(5)]
    last0 = line_gram(1, rows - 2, 0)
    zero0 = [sums[0]]
    zero0.append(zero0[0] + last0)
    zero0.append(zero0[1] + line_gram(1, rows - 1, 0))
    zero0.append(zero0[2] - line_gram(0, 0, 0))
    zero0.append(zero0[3] - line_gram(0, 1, 0))
    one = [sums[1]]
    one.append(one[0] + line_gram(1, rows - 2, 1))
    one.append(one[1])
    one.append(one[1] - line_gram(0, 0, 1))

    row_i = lax.broadcasted_iota(jnp.int32, (size, size), 0)
    col_i = lax.broadcasted_iota(jnp.int32, (size, size), 1)
    per_frame = size // (2 * frames)
    row_frame = row_i // per_frame % frames
    col_frame = col_i // per_frame % frames
    col_part = col_i // (size // 2)
    weight = jnp.zeros((size, size), jnp.float32)
    for s in range(frames):
        reach = sum(1 for t in range(frames) if abs(s - t) <= 2)
        weight = jnp.where(row_frame == s, float(reach), weight)
    diagonal = zero0[0] + zero0[1] + zero0[2] + zero0[3] + zero0[4]
    diagonal = jnp.where(row_i == col_i, diagonal * weight, 0.0)
    trace = jnp.sum(jnp.sum(diagonal, axis=0, keepdims=True), axis=1, keepdims=True)
    scale = trace / (125 * coils) + 1e-06

    table = couplings(frames)
    half = size // 2

    def lane_roll(x, by):
        by = by % size
        return x if by == 0 else jnp.concatenate([x[:, size - by :], x[:, : size - by]], axis=1)

    def mixed(raw):
        swapped = lane_roll(raw, half)
        sign = jnp.where(col_part[:half] == 0, 1.0, -1.0)
        whole = jnp.concatenate(
            [raw[:half] + sign * swapped[half:], raw[half:] - sign * swapped[:half]], axis=0
        )
        result = jnp.zeros_like(whole)
        for d in range(1 - frames, frames):
            terms = {k: v for k, v in table.items() if k[2] == d}
            if not terms:
                continue
            by = d * per_frame
            moved = lane_roll(whole, -by)
            if by % size:
                moved = jnp.concatenate([moved[by % size :], moved[: by % size]], axis=0)
            factor = jnp.zeros_like(whole)
            for (s, s2, _), v in terms.items():
                factor = jnp.where((row_frame == s) & (col_frame == s2), float(v), factor)
            result = result + factor * moved
        return result

    def put(row, col, x):
        hi, lo = halves(x)
        m_hi[col, pl.ds(row * size, size), :] = hi
        m_lo[col, pl.ds(row * size, size), :] = lo

    for b in range(5):
        put(b, b, mixed(zero0[b]))
    kept = None
    for b in range(4):
        if b != 2:
            kept = mixed(one[b])
            turned = kept.T
        put(b + 1, b, kept)
        put(b, b + 1, turned)
    for dy in range(2, 5):
        kept = mixed(sums[dy])
        turned = kept.T
        for b in range(5 - dy):
            put(b + dy, b, kept)
            put(b, b + dy, turned)

    wide = 2 * LANES
    ext = window(me, 4, 4 * LANES)
    cell = lax.broadcasted_iota(jnp.int32, (1, wide), 1)
    line = cell // stride + me * rows - 2
    usable = (cell % stride < readout) & (cell < (rows + 4) * stride)
    usable = usable & (line >= 0) & (line < total)
    for b in range(5):
        hi, lo = halves(jnp.where(usable, shifted(ext, b, wide), 0.0))
        p_hi[b] = hi
        p_lo[b] = lo
    folded = jnp.zeros((channels, LANES), jnp.float32)
    for b2 in range(5):
        at = pl.ds(b2 * size, size)
        piece = jnp.zeros((size, wide), jnp.float32)
        for b in range(5):
            piece = piece + (
                dot_nn(m_hi[b, at, :], p_hi[b])
                + dot_nn(m_hi[b, at, :], p_lo[b])
                + dot_nn(m_lo[b, at, :], p_hi[b])
            )
        for e in range(5):
            part = jnp.concatenate(
                [
                    piece[(g * 5 + e) * coils : (g * 5 + e + 1) * coils]
                    for g in range(2 * frames)
                ],
                axis=0,
            )
            by = (-((4 - b2) * stride + 2 - e)) % wide
            folded = folded + (pltpu.roll(part, by, 1) if by else part)[:, :LANES]
    out_ref[...] = folded / (125.0 * scale)


def local(estimate, measured, sampled_lines):
    _, coils, frames, rows, readout = estimate.shape
    n = lax.axis_size("slab")
    place = lax.axis_index("slab")
    stride = readout + 4
    channels = 2 * frames * coils
    size = 5 * channels
    cells = jnp.transpose(estimate, (0, 2, 1, 3, 4)).reshape(channels, rows, readout)
    cells = jnp.pad(cells, ((0, 0), (0, 0), (2, 2))).reshape(channels, rows * stride)
    block = jnp.pad(cells, ((0, 0), (0, LANES - rows * stride)))
    everything = gathered(block, n)
    chunk = max(k for k in range(1, min(n, 16) + 1) if n % k == 0)
    depth = chunk * LANES
    bf16 = jnp.bfloat16
    folded = pl.pallas_call(
        functools.partial(filter_kernel, n, chunk, frames, coils, rows, readout),
        out_shape=jax.ShapeDtypeStruct((channels, LANES), jnp.float32),
        in_specs=[pl.BlockSpec(memory_space=pltpu.VMEM)],
        out_specs=pl.BlockSpec(memory_space=pltpu.VMEM),
        scratch_shapes=[
            pltpu.VMEM((5 * size, depth), bf16),
            pltpu.VMEM((5 * size, depth), bf16),
            pltpu.VMEM((size, depth), bf16),
            pltpu.VMEM((size, depth), bf16),
            pltpu.VMEM((4, size, LANES), bf16),
            pltpu.VMEM((4, size, LANES), bf16),
            pltpu.VMEM((5, size, 2 * LANES), bf16),
            pltpu.VMEM((5, size, 2 * LANES), bf16),
            pltpu.VMEM((5, 5 * size, size), bf16),
            pltpu.VMEM((5, 5 * size, size), bf16),
            pltpu.VMEM((5 * size, size), jnp.float32),
        ],
        compiler_params=pltpu.CompilerParams(vmem_limit_bytes=48 * 1024 * 1024),
    )(everything)
    folded = folded[:, : rows * stride].reshape(2, frames, coils, rows, stride)[..., :readout]
    folded = jnp.transpose(folded, (0, 2, 1, 3, 4))
    line_index = place * rows + jnp.arange(rows, dtype=jnp.int32)
    hit = jnp.any(sampled_lines[:, :, None] == line_index[None, None, :], axis=1)
    return jnp.where(hit[None, None, :, :, None], measured, folded)


def solution(mesh):
    placed = (
        P(None, None, "grp", "slab", None),
        P(None, None, "grp", "slab", None),
        P("grp", None),
    )
    return jax.shard_map(
        local,
        mesh=mesh,
        in_specs=placed,
        out_specs=P(None, None, "grp", "slab", None),
        check_vma=False,
    )
```

```python
import functools

import jax
import jax.numpy as jnp
from jax import lax
from jax.experimental import pallas as pl
from jax.experimental.pallas import tpu as pltpu
from jax.sharding import PartitionSpec as P

LANES = 128


def gather_kernel(n, x_ref, out_ref, send_sem, recv_sem, own_sem):
    me = lax.axis_index("slab")

    def greet(k, carry):
        pl.semaphore_signal(
            pltpu.get_barrier_semaphore(), inc=1, device_id={"slab": lax.rem(me + k, n)}
        )
        return carry

    lax.fori_loop(1, n, greet, 0)
    own = pltpu.make_async_copy(x_ref, out_ref.at[me], own_sem)
    own.start()
    pl.semaphore_wait(pltpu.get_barrier_semaphore(), n - 1)

    def copy(k, place):
        return pltpu.make_async_remote_copy(
            src_ref=x_ref,
            dst_ref=out_ref.at[place],
            send_sem=send_sem.at[k - 1],
            recv_sem=recv_sem.at[k - 1],
            device_id={"slab": lax.rem(me + k, n)},
        )

    def send(k, carry):
        copy(k, me).start()
        return carry

    def receive(k, carry):
        copy(k, lax.rem(me + n - k, n)).wait_recv()
        return carry

    def finish(k, carry):
        copy(k, me).wait_send()
        return carry

    lax.fori_loop(1, n, send, 0)
    own.wait()
    lax.fori_loop(1, n, receive, 0)
    lax.fori_loop(1, n, finish, 0)


def gathered(block, n):
    return pl.pallas_call(
        functools.partial(gather_kernel, n),
        out_shape=jax.ShapeDtypeStruct((n,) + block.shape, block.dtype),
        in_specs=[pl.BlockSpec(memory_space=pltpu.VMEM)],
        out_specs=pl.BlockSpec(memory_space=pltpu.VMEM),
        scratch_shapes=[
            pltpu.SemaphoreType.DMA((n - 1,)),
            pltpu.SemaphoreType.DMA((n - 1,)),
            pltpu.SemaphoreType.DMA,
        ],
        compiler_params=pltpu.CompilerParams(collective_id=0, has_side_effects=True),
    )(block)


def couplings(frames):
    table = {}
    for s in range(frames):
        for s2 in range(frames):
            for d in range(1 - frames, frames):
                if 0 <= s + d < frames and 0 <= s2 + d < frames:
                    n = sum(
                        1
                        for t in range(frames)
                        if 0 <= t + d < frames and abs(s - t) <= 2 and abs(s2 - t) <= 2
                    )
                    if n:
                        table[s, s2, d] = n
    return table


def halves(x):
    hi = x.astype(jnp.bfloat16)
    return hi, (x - hi.astype(jnp.float32)).astype(jnp.bfloat16)


def dot_nt(a, b):
    return lax.dot_general(a, b, (((1,), (1,)), ((), ())), preferred_element_type=jnp.float32)


def dot_nn(a, b):
    return lax.dot_general(a, b, (((1,), (0,)), ((), ())), preferred_element_type=jnp.float32)


def filter_kernel(n, frames, coils, rows, readout, all_ref, out_ref, *scratch):
    q_hi, q_lo, l_hi, l_lo, p_hi, p_lo, m_hi, m_lo = scratch
    me = lax.axis_index("slab")
    stride = readout + 4
    fit = LANES // stride
    channels = 2 * frames * coils
    size = 5 * channels
    total = n * rows
    deep = -(-total // fit)
    near = -(-(rows + 4) // fit)
    lane = lax.broadcasted_iota(jnp.int32, (1, LANES), 1)
    slot = lane // stride
    valid = (lane % stride < readout) & (slot < fit)

    def tile(lines):
        result = jnp.zeros((channels, LANES), jnp.float32)
        for g, source in enumerate(lines):
            if source is not None:
                block, j = source
                by = (g - j) * stride % LANES
                moved = pltpu.roll(block, by, 1) if by else block
                result = jnp.where(slot == g, moved, result)
        return result

    def spread(cells):
        moved = [pltpu.roll(cells, LANES - e, 1) if e else cells for e in range(5)]
        return jnp.concatenate(
            [
                moved[e][g * coils : (g + 1) * coils]
                for g in range(2 * frames)
                for e in range(5)
            ],
            axis=0,
        )

    for k in range(deep + 4):
        lines = []
        for g in range(fit):
            line = k + deep * g
            lines.append((all_ref[line // rows], line % rows) if line < total else None)
        hi, lo = halves(spread(tile(lines)))
        at = pl.ds(k * LANES, LANES)
        q_hi[:, at] = hi
        q_lo[:, at] = lo
        if k < deep:
            l_hi[:, at] = jnp.where(valid, hi, jnp.zeros_like(hi))
            l_lo[:, at] = jnp.where(valid, lo, jnp.zeros_like(lo))

    for k in range(near + 4):
        lines = []
        for g in range(fit):
            line = k + near * g - 4
            other = me + line // rows
            block = all_ref[jnp.clip(other, 0, n - 1)]
            lines.append((jnp.where((other >= 0) & (other < n), block, 0.0), line % rows))
        hi, lo = halves(spread(tile(lines)))
        p_hi[:, pl.ds(k * LANES, LANES)] = hi
        p_lo[:, pl.ds(k * LANES, LANES)] = lo

    def gram(first, count, dy):
        left = pl.ds(first * LANES, count * LANES)
        right = pl.ds((first + dy) * LANES, count * LANES)
        return (
            dot_nt(q_hi[:, right], l_hi[:, left])
            + dot_nt(q_hi[:, right], l_lo[:, left])
            + dot_nt(q_lo[:, right], l_hi[:, left])
        )

    def line_gram(line, dy):
        left = pl.ds(line % deep * LANES, LANES)
        right = pl.ds((line % deep + dy) * LANES, LANES)
        pick = slot == line // deep
        hi = jnp.where(pick, l_hi[:, left], 0)
        lo = jnp.where(pick, l_lo[:, left], 0)
        return dot_nt(q_hi[:, right], hi) + dot_nt(q_hi[:, right], lo) + dot_nt(q_lo[:, right], hi)

    step = 16
    sums = []
    for dy in range(5):
        sofar = None
        for first in range(0, deep, step):
            term = gram(first, min(step, deep - first), dy)
            sofar = term if sofar is None else sofar + term
        sums.append(sofar)

    zero0 = [None, None, sums[0]]
    zero0[1] = sums[0] - line_gram(total - 1, 0)
    zero0[0] = zero0[1] - line_gram(total - 2, 0)
    zero0.append(sums[0] - line_gram(0, 0))
    zero0.append(zero0[3] - line_gram(1, 0))
    one = [sums[1] - line_gram(total - 2, 1), sums[1], sums[1], sums[1] - line_gram(0, 1)]

    row_i = lax.broadcasted_iota(jnp.int32, (size, size), 0)
    col_i = lax.broadcasted_iota(jnp.int32, (size, size), 1)
    per_frame = size // (2 * frames)
    row_frame = row_i // per_frame % frames
    col_frame = col_i // per_frame % frames
    col_part = col_i // (size // 2)
    weight = jnp.zeros((size, size), jnp.float32)
    for s in range(frames):
        reach = sum(1 for t in range(frames) if abs(s - t) <= 2)
        weight = jnp.where(row_frame == s, float(reach), weight)
    diagonal = zero0[0] + zero0[1] + zero0[2] + zero0[3] + zero0[4]
    diagonal = jnp.where(row_i == col_i, diagonal * weight, 0.0)
    trace = jnp.sum(jnp.sum(diagonal, axis=0, keepdims=True), axis=1, keepdims=True)
    scale = trace / (125 * coils) + 1e-06

    table = couplings(frames)
    half = size // 2

    def lane_roll(x, by):
        by = by % size
        return x if by == 0 else jnp.concatenate([x[:, size - by :], x[:, : size - by]], axis=1)

    def mixed(raw):
        swapped = lane_roll(raw, half)
        sign = jnp.where(col_part[:half] == 0, 1.0, -1.0)
        whole = jnp.concatenate(
            [raw[:half] + sign * swapped[half:], raw[half:] - sign * swapped[:half]], axis=0
        )
        result = jnp.zeros_like(whole)
        for d in range(1 - frames, frames):
            terms = {k: v for k, v in table.items() if k[2] == d}
            if not terms:
                continue
            by = d * per_frame
            moved = lane_roll(whole, -by)
            if by % size:
                moved = jnp.concatenate([moved[by % size :], moved[: by % size]], axis=0)
            factor = jnp.zeros_like(whole)
            for (s, s2, _), v in terms.items():
                factor = jnp.where((row_frame == s) & (col_frame == s2), float(v), factor)
            result = result + factor * moved
        return result

    def put(row, col, x):
        hi, lo = halves(x)
        m_hi[col, pl.ds(row * size, size), :] = hi
        m_lo[col, pl.ds(row * size, size), :] = lo

    for b in range(5):
        put(b, b, mixed(zero0[b]))
    kept = None
    for b in range(4):
        if b != 2:
            kept = mixed(one[b])
            turned = kept.T
        put(b + 1, b, kept)
        put(b, b + 1, turned)
    for dy in range(2, 5):
        kept = mixed(sums[dy])
        turned = kept.T
        for b in range(5 - dy):
            put(b + dy, b, kept)
            put(b, b + dy, turned)

    wide = near * LANES
    cell = lax.broadcasted_iota(jnp.int32, (1, wide), 1)
    cell_slot = cell % LANES // stride
    line = cell // LANES + near * cell_slot
    usable = (cell % LANES % stride < readout) & (cell_slot < fit) & (line < rows + 4)
    line = line + me * rows - 2
    usable = usable & (line >= 0) & (line < total)
    gathers = {}
    for b2 in range(5):
        at = pl.ds(b2 * size, size)
        piece = jnp.zeros((size, wide), jnp.float32)
        for b in range(5):
            cols = pl.ds(b * LANES, wide)
            piece = piece + (
                dot_nn(m_hi[b, at, :], p_hi[:, cols])
                + dot_nn(m_hi[b, at, :], p_lo[:, cols])
                + dot_nn(m_lo[b, at, :], p_hi[:, cols])
            )
        piece = jnp.where(usable, piece, 0.0)
        for e in range(5):
            part = jnp.concatenate(
                [
                    piece[(g * 5 + e) * coils : (g * 5 + e + 1) * coils]
                    for g in range(2 * frames)
                ],
                axis=0,
            )
            for j in range(rows):
                line = j - b2 + 4
                k, g = line % near, line // near
                term = jnp.where(slot == g, part[:, k * LANES : (k + 1) * LANES], 0.0)
                key = (e, j - g)
                gathers[key] = gathers[key] + term if key in gathers else term
    folded = jnp.zeros((channels, LANES), jnp.float32)
    for (e, moves), term in gathers.items():
        by = (moves * stride + e - 2) % LANES
        folded = folded + (pltpu.roll(term, by, 1) if by else term)
    out_ref[...] = folded / (125.0 * scale)


def local(estimate, measured, sampled_lines):
    _, coils, frames, rows, readout = estimate.shape
    n = lax.axis_size("slab")
    place = lax.axis_index("slab")
    stride = readout + 4
    channels = 2 * frames * coils
    size = 5 * channels
    cells = jnp.transpose(estimate, (0, 2, 1, 3, 4)).reshape(channels, rows, readout)
    cells = jnp.pad(cells, ((0, 0), (0, 0), (2, 2))).reshape(channels, rows * stride)
    block = jnp.pad(cells, ((0, 0), (0, LANES - rows * stride)))
    everything = gathered(block, n)
    fit = LANES // stride
    deep = -(-n * rows // fit) * LANES
    near = -(-(rows + 4) // fit) * LANES
    bf16 = jnp.bfloat16
    folded = pl.pallas_call(
        functools.partial(filter_kernel, n, frames, coils, rows, readout),
        out_shape=jax.ShapeDtypeStruct((channels, LANES), jnp.float32),
        in_specs=[pl.BlockSpec(memory_space=pltpu.VMEM)],
        out_specs=pl.BlockSpec(memory_space=pltpu.VMEM),
        scratch_shapes=[
            pltpu.VMEM((size, deep + 4 * LANES), bf16),
            pltpu.VMEM((size, deep + 4 * LANES), bf16),
            pltpu.VMEM((size, deep), bf16),
            pltpu.VMEM((size, deep), bf16),
            pltpu.VMEM((size, near + 4 * LANES), bf16),
            pltpu.VMEM((size, near + 4 * LANES), bf16),
            pltpu.VMEM((5, 5 * size, size), bf16),
            pltpu.VMEM((5, 5 * size, size), bf16),
        ],
        compiler_params=pltpu.CompilerParams(vmem_limit_bytes=48 * 1024 * 1024),
    )(everything)
    folded = folded[:, : rows * stride].reshape(2, frames, coils, rows, stride)[..., :readout]
    folded = jnp.transpose(folded, (0, 2, 1, 3, 4))
    line_index = place * rows + jnp.arange(rows, dtype=jnp.int32)
    hit = jnp.any(sampled_lines[:, :, None] == line_index[None, None, :], axis=1)
    return jnp.where(hit[None, None, :, :, None], measured, folded)


def solution(mesh):
    placed = (
        P(None, None, "grp", "slab", None),
        P(None, None, "grp", "slab", None),
        P("grp", None),
    )
    return jax.shard_map(
        local,
        mesh=mesh,
        in_specs=placed,
        out_specs=P(None, None, "grp", "slab", None),
        check_vma=False,
    )
```

```python
import functools

import jax
import jax.numpy as jnp
from jax import lax
from jax.experimental import pallas as pl
from jax.experimental.pallas import tpu as pltpu
from jax.sharding import PartitionSpec as P

LANES = 128


def gather_kernel(n, x_ref, out_ref, send_sem, recv_sem, own_sem):
    me = lax.axis_index("slab")

    def greet(k, carry):
        pl.semaphore_signal(
            pltpu.get_barrier_semaphore(), inc=1, device_id={"slab": lax.rem(me + k, n)}
        )
        return carry

    lax.fori_loop(1, n, greet, 0)
    own = pltpu.make_async_copy(x_ref, out_ref.at[me], own_sem)
    own.start()
    pl.semaphore_wait(pltpu.get_barrier_semaphore(), n - 1)

    def copy(k, place):
        return pltpu.make_async_remote_copy(
            src_ref=x_ref,
            dst_ref=out_ref.at[place],
            send_sem=send_sem.at[k - 1],
            recv_sem=recv_sem.at[k - 1],
            device_id={"slab": lax.rem(me + k, n)},
        )

    def send(k, carry):
        copy(k, me).start()
        return carry

    def receive(k, carry):
        copy(k, lax.rem(me + n - k, n)).wait_recv()
        return carry

    def finish(k, carry):
        copy(k, me).wait_send()
        return carry

    lax.fori_loop(1, n, send, 0)
    own.wait()
    lax.fori_loop(1, n, receive, 0)
    lax.fori_loop(1, n, finish, 0)


def whole_kernel(n, sizes, x_ref, out_ref, all_ref, send_sem, recv_sem, own_sem, *scratch):
    gather_kernel(n, x_ref, all_ref, send_sem, recv_sem, own_sem)
    filter_kernel(n, *sizes, all_ref, out_ref, *scratch)


def couplings(frames):
    table = {}
    for s in range(frames):
        for s2 in range(frames):
            for d in range(1 - frames, frames):
                if 0 <= s + d < frames and 0 <= s2 + d < frames:
                    n = sum(
                        1
                        for t in range(frames)
                        if 0 <= t + d < frames and abs(s - t) <= 2 and abs(s2 - t) <= 2
                    )
                    if n:
                        table[s, s2, d] = n
    return table


def halves(x):
    hi = x.astype(jnp.bfloat16)
    return hi, (x - hi.astype(jnp.float32)).astype(jnp.bfloat16)


def dot_nt(a, b):
    return lax.dot_general(a, b, (((1,), (1,)), ((), ())), preferred_element_type=jnp.float32)


def dot_nn(a, b):
    return lax.dot_general(a, b, (((1,), (0,)), ((), ())), preferred_element_type=jnp.float32)


def filter_kernel(n, frames, coils, rows, readout, all_ref, out_ref, *scratch):
    q_hi, q_lo, l_hi, l_lo, p_hi, p_lo, m_hi, m_lo = scratch
    me = lax.axis_index("slab")
    stride = readout + 4
    fit = LANES // stride
    channels = 2 * frames * coils
    size = 5 * channels
    total = n * rows
    deep = -(-total // fit)
    near = -(-(rows + 4) // fit)
    lane = lax.broadcasted_iota(jnp.int32, (1, LANES), 1)
    slot = lane // stride
    valid = (lane % stride < readout) & (slot < fit)

    def tile(lines):
        result = jnp.zeros((channels, LANES), jnp.float32)
        for g, source in enumerate(lines):
            if source is not None:
                block, j = source
                by = (g - j) * stride % LANES
                moved = pltpu.roll(block, by, 1) if by else block
                result = jnp.where(slot == g, moved, result)
        return result

    def spread(cells):
        moved = [pltpu.roll(cells, LANES - e, 1) if e else cells for e in range(5)]
        return jnp.concatenate(
            [
                moved[e][g * coils : (g + 1) * coils]
                for g in range(2 * frames)
                for e in range(5)
            ],
            axis=0,
        )

    for k in range(deep + 4):
        lines = []
        for g in range(fit):
            line = k + deep * g
            lines.append((all_ref[line // rows], line % rows) if line < total else None)
        hi, lo = halves(spread(tile(lines)))
        at = pl.ds(k * LANES, LANES)
        q_hi[:, at] = hi
        q_lo[:, at] = lo
        if k < deep:
            l_hi[:, at] = jnp.where(valid, hi, jnp.zeros_like(hi))
            l_lo[:, at] = jnp.where(valid, lo, jnp.zeros_like(lo))

    for k in range(near + 4):
        lines = []
        for g in range(fit):
            line = k + near * g - 4
            other = me + line // rows
            block = all_ref[jnp.clip(other, 0, n - 1)]
            lines.append((jnp.where((other >= 0) & (other < n), block, 0.0), line % rows))
        hi, lo = halves(spread(tile(lines)))
        p_hi[:, pl.ds(k * LANES, LANES)] = hi
        p_lo[:, pl.ds(k * LANES, LANES)] = lo

    def gram(first, count, dy):
        left = pl.ds(first * LANES, count * LANES)
        right = pl.ds((first + dy) * LANES, count * LANES)
        return (
            dot_nt(q_hi[:, right], l_hi[:, left])
            + dot_nt(q_hi[:, right], l_lo[:, left])
            + dot_nt(q_lo[:, right], l_hi[:, left])
        )

    def line_gram(line, dy):
        left = pl.ds(line % deep * LANES, LANES)
        right = pl.ds((line % deep + dy) * LANES, LANES)
        pick = slot == line // deep
        hi = jnp.where(pick, l_hi[:, left], 0)
        lo = jnp.where(pick, l_lo[:, left], 0)
        return dot_nt(q_hi[:, right], hi) + dot_nt(q_hi[:, right], lo) + dot_nt(q_lo[:, right], hi)

    step = 16
    sums = []
    for dy in range(5):
        sofar = None
        for first in range(0, deep, step):
            term = gram(first, min(step, deep - first), dy)
            sofar = term if sofar is None else sofar + term
        sums.append(sofar)

    zero0 = [None, None, sums[0]]
    zero0[1] = sums[0] - line_gram(total - 1, 0)
    zero0[0] = zero0[1] - line_gram(total - 2, 0)
    zero0.append(sums[0] - line_gram(0, 0))
    zero0.append(zero0[3] - line_gram(1, 0))
    one = [sums[1] - line_gram(total - 2, 1), sums[1], sums[1], sums[1] - line_gram(0, 1)]

    row_i = lax.broadcasted_iota(jnp.int32, (size, size), 0)
    col_i = lax.broadcasted_iota(jnp.int32, (size, size), 1)
    per_frame = size // (2 * frames)
    row_frame = row_i // per_frame % frames
    col_frame = col_i // per_frame % frames
    col_part = col_i // (size // 2)
    weight = jnp.zeros((size, size), jnp.float32)
    for s in range(frames):
        reach = sum(1 for t in range(frames) if abs(s - t) <= 2)
        weight = jnp.where(row_frame == s, float(reach), weight)
    diagonal = zero0[0] + zero0[1] + zero0[2] + zero0[3] + zero0[4]
    diagonal = jnp.where(row_i == col_i, diagonal * weight, 0.0)
    trace = jnp.sum(jnp.sum(diagonal, axis=0, keepdims=True), axis=1, keepdims=True)
    scale = trace / (125 * coils) + 1e-06

    table = couplings(frames)
    half = size // 2

    def lane_roll(x, by):
        by = by % size
        return x if by == 0 else jnp.concatenate([x[:, size - by :], x[:, : size - by]], axis=1)

    def mixed(raw):
        swapped = lane_roll(raw, half)
        sign = jnp.where(col_part[:half] == 0, 1.0, -1.0)
        whole = jnp.concatenate(
            [raw[:half] + sign * swapped[half:], raw[half:] - sign * swapped[:half]], axis=0
        )
        result = jnp.zeros_like(whole)
        for d in range(1 - frames, frames):
            terms = {k: v for k, v in table.items() if k[2] == d}
            if not terms:
                continue
            by = d * per_frame
            moved = lane_roll(whole, -by)
            if by % size:
                moved = jnp.concatenate([moved[by % size :], moved[: by % size]], axis=0)
            factor = jnp.zeros_like(whole)
            for (s, s2, _), v in terms.items():
                factor = jnp.where((row_frame == s) & (col_frame == s2), float(v), factor)
            result = result + factor * moved
        return result

    def put(row, col, x):
        hi, lo = halves(x)
        m_hi[col, pl.ds(row * size, size), :] = hi
        m_lo[col, pl.ds(row * size, size), :] = lo

    for b in range(5):
        put(b, b, mixed(zero0[b]))
    kept = None
    for b in range(4):
        if b != 2:
            kept = mixed(one[b])
            turned = kept.T
        put(b + 1, b, kept)
        put(b, b + 1, turned)
    for dy in range(2, 5):
        kept = mixed(sums[dy])
        turned = kept.T
        for b in range(5 - dy):
            put(b + dy, b, kept)
            put(b, b + dy, turned)

    wide = near * LANES
    cell = lax.broadcasted_iota(jnp.int32, (1, wide), 1)
    cell_slot = cell % LANES // stride
    line = cell // LANES + near * cell_slot
    usable = (cell % LANES % stride < readout) & (cell_slot < fit) & (line < rows + 4)
    line = line + me * rows - 2
    usable = usable & (line >= 0) & (line < total)
    gathers = {}
    for b2 in range(5):
        at = pl.ds(b2 * size, size)
        piece = jnp.zeros((size, wide), jnp.float32)
        for b in range(5):
            cols = pl.ds(b * LANES, wide)
            piece = piece + (
                dot_nn(m_hi[b, at, :], p_hi[:, cols])
                + dot_nn(m_hi[b, at, :], p_lo[:, cols])
                + dot_nn(m_lo[b, at, :], p_hi[:, cols])
            )
        piece = jnp.where(usable, piece, 0.0)
        for e in range(5):
            part = jnp.concatenate(
                [
                    piece[(g * 5 + e) * coils : (g * 5 + e + 1) * coils]
                    for g in range(2 * frames)
                ],
                axis=0,
            )
            for j in range(rows):
                line = j - b2 + 4
                k, g = line % near, line // near
                term = jnp.where(slot == g, part[:, k * LANES : (k + 1) * LANES], 0.0)
                key = (e, j - g)
                gathers[key] = gathers[key] + term if key in gathers else term
    folded = jnp.zeros((channels, LANES), jnp.float32)
    for (e, moves), term in gathers.items():
        by = (moves * stride + e - 2) % LANES
        folded = folded + (pltpu.roll(term, by, 1) if by else term)
    out_ref[...] = folded / (125.0 * scale)


def local(estimate, measured, sampled_lines):
    _, coils, frames, rows, readout = estimate.shape
    n = lax.axis_size("slab")
    place = lax.axis_index("slab")
    stride = readout + 4
    channels = 2 * frames * coils
    size = 5 * channels
    cells = jnp.transpose(estimate, (0, 2, 1, 3, 4)).reshape(channels, rows, readout)
    cells = jnp.pad(cells, ((0, 0), (0, 0), (2, 2))).reshape(channels, rows * stride)
    block = jnp.pad(cells, ((0, 0), (0, LANES - rows * stride)))
    fit = LANES // stride
    deep = -(-n * rows // fit) * LANES
    near = -(-(rows + 4) // fit) * LANES
    bf16 = jnp.bfloat16
    folded = pl.pallas_call(
        functools.partial(whole_kernel, n, (frames, coils, rows, readout)),
        out_shape=jax.ShapeDtypeStruct((channels, LANES), jnp.float32),
        in_specs=[pl.BlockSpec(memory_space=pltpu.VMEM)],
        out_specs=pl.BlockSpec(memory_space=pltpu.VMEM),
        scratch_shapes=[
            pltpu.VMEM((n, channels, LANES), jnp.float32),
            pltpu.SemaphoreType.DMA((n,)),
            pltpu.SemaphoreType.DMA((n,)),
            pltpu.SemaphoreType.DMA,
            pltpu.VMEM((size, deep + 4 * LANES), bf16),
            pltpu.VMEM((size, deep + 4 * LANES), bf16),
            pltpu.VMEM((size, deep), bf16),
            pltpu.VMEM((size, deep), bf16),
            pltpu.VMEM((size, near + 4 * LANES), bf16),
            pltpu.VMEM((size, near + 4 * LANES), bf16),
            pltpu.VMEM((5, 5 * size, size), bf16),
            pltpu.VMEM((5, 5 * size, size), bf16),
        ],
        compiler_params=pltpu.CompilerParams(
            vmem_limit_bytes=48 * 1024 * 1024, collective_id=0, has_side_effects=True
        ),
    )(block)
    folded = folded[:, : rows * stride].reshape(2, frames, coils, rows, stride)[..., :readout]
    folded = jnp.transpose(folded, (0, 2, 1, 3, 4))
    line_index = place * rows + jnp.arange(rows, dtype=jnp.int32)
    hit = jnp.any(sampled_lines[:, :, None] == line_index[None, None, :], axis=1)
    return jnp.where(hit[None, None, :, :, None], measured, folded)


def solution(mesh):
    placed = (
        P(None, None, "grp", "slab", None),
        P(None, None, "grp", "slab", None),
        P("grp", None),
    )
    return jax.shard_map(
        local,
        mesh=mesh,
        in_specs=placed,
        out_specs=P(None, None, "grp", "slab", None),
        check_vma=False,
    )
```

```python
import functools

import jax
import jax.numpy as jnp
from jax import lax
from jax.experimental import pallas as pl
from jax.experimental.pallas import tpu as pltpu
from jax.sharding import PartitionSpec as P

LANES = 128


def gather_kernel(n, reach, early, x_ref, out_ref, send_sem, recv_sem, own_sem):
    me = lax.axis_index("slab")

    def greet(k, carry):
        pl.semaphore_signal(
            pltpu.get_barrier_semaphore(), inc=1, device_id={"slab": lax.rem(me + k, n)}
        )
        return carry

    lax.fori_loop(1, n, greet, 0)
    own = pltpu.make_async_copy(x_ref, out_ref.at[me], own_sem)
    own.start()
    pl.semaphore_wait(pltpu.get_barrier_semaphore(), n - 1)

    def copy(k, place):
        return pltpu.make_async_remote_copy(
            src_ref=x_ref,
            dst_ref=out_ref.at[place],
            send_sem=send_sem.at[k - 1],
            recv_sem=recv_sem.at[k - 1],
            device_id={"slab": lax.rem(me + k, n)},
        )

    def send(k, carry):
        copy(k, me).start()
        return carry

    def receive(k, carry):
        copy(k, lax.rem(me + n - k, n)).wait_recv()
        return carry

    def finish(k, carry):
        copy(k, me).wait_send()
        return carry

    lax.fori_loop(1, n, send, 0)
    own.wait()
    for k in (*range(1, reach + 1), *range(n - reach, n)):
        receive(k, 0)
    early()
    lax.fori_loop(reach + 1, n - reach, receive, 0)
    lax.fori_loop(1, n, finish, 0)


def whole_kernel(n, sizes, x_ref, out_ref, all_ref, send_sem, recv_sem, own_sem, *scratch):
    def gather(reach, early):
        gather_kernel(n, reach, early, x_ref, all_ref, send_sem, recv_sem, own_sem)

    filter_kernel(n, gather, *sizes, all_ref, out_ref, *scratch)


def couplings(frames):
    table = {}
    for s in range(frames):
        for s2 in range(frames):
            for d in range(1 - frames, frames):
                if 0 <= s + d < frames and 0 <= s2 + d < frames:
                    n = sum(
                        1
                        for t in range(frames)
                        if 0 <= t + d < frames and abs(s - t) <= 2 and abs(s2 - t) <= 2
                    )
                    if n:
                        table[s, s2, d] = n
    return table


def halves(x):
    hi = x.astype(jnp.bfloat16)
    return hi, (x - hi.astype(jnp.float32)).astype(jnp.bfloat16)


def dot_nt(a, b):
    return lax.dot_general(a, b, (((1,), (1,)), ((), ())), preferred_element_type=jnp.float32)


def dot_nn(a, b):
    return lax.dot_general(a, b, (((1,), (0,)), ((), ())), preferred_element_type=jnp.float32)


def filter_kernel(n, gather, frames, coils, rows, readout, all_ref, out_ref, *scratch):
    q_hi, q_lo, l_hi, l_lo, p_hi, p_lo, m_hi, m_lo = scratch
    me = lax.axis_index("slab")
    stride = readout + 4
    fit = LANES // stride
    channels = 2 * frames * coils
    size = 5 * channels
    total = n * rows
    deep = -(-total // fit)
    near = -(-(rows + 4) // fit)
    lane = lax.broadcasted_iota(jnp.int32, (1, LANES), 1)
    slot = lane // stride
    valid = (lane % stride < readout) & (slot < fit)

    def tile(lines):
        result = jnp.zeros((channels, LANES), jnp.float32)
        for g, source in enumerate(lines):
            if source is not None:
                block, j = source
                by = (g - j) * stride % LANES
                moved = pltpu.roll(block, by, 1) if by else block
                result = jnp.where(slot == g, moved, result)
        return result

    def spread(cells):
        moved = [pltpu.roll(cells, LANES - e, 1) if e else cells for e in range(5)]
        return jnp.concatenate(
            [
                moved[e][g * coils : (g + 1) * coils]
                for g in range(2 * frames)
                for e in range(5)
            ],
            axis=0,
        )

    def build_near():
        for k in range(near + 4):
            lines = []
            for g in range(fit):
                line = k + near * g - 4
                other = me + line // rows
                block = all_ref[jnp.clip(other, 0, n - 1)]
                lines.append((jnp.where((other >= 0) & (other < n), block, 0.0), line % rows))
            hi, lo = halves(spread(tile(lines)))
            p_hi[:, pl.ds(k * LANES, LANES)] = hi
            p_lo[:, pl.ds(k * LANES, LANES)] = lo

    gather(max(-(-4 // rows), (near * fit - 1) // rows), build_near)

    for k in range(deep + 4):
        lines = []
        for g in range(fit):
            line = k + deep * g
            lines.append((all_ref[line // rows], line % rows) if line < total else None)
        hi, lo = halves(spread(tile(lines)))
        at = pl.ds(k * LANES, LANES)
        q_hi[:, at] = hi
        q_lo[:, at] = lo
        if k < deep:
            l_hi[:, at] = jnp.where(valid, hi, jnp.zeros_like(hi))
            l_lo[:, at] = jnp.where(valid, lo, jnp.zeros_like(lo))

    def gram(first, count, dy):
        left = pl.ds(first * LANES, count * LANES)
        right = pl.ds((first + dy) * LANES, count * LANES)
        return (
            dot_nt(q_hi[:, right], l_hi[:, left])
            + dot_nt(q_hi[:, right], l_lo[:, left])
            + dot_nt(q_lo[:, right], l_hi[:, left])
        )

    def line_gram(line, dy):
        left = pl.ds(line % deep * LANES, LANES)
        right = pl.ds((line % deep + dy) * LANES, LANES)
        pick = slot == line // deep
        hi = jnp.where(pick, l_hi[:, left], 0)
        lo = jnp.where(pick, l_lo[:, left], 0)
        return dot_nt(q_hi[:, right], hi) + dot_nt(q_hi[:, right], lo) + dot_nt(q_lo[:, right], hi)

    step = 16
    sums = []
    for dy in range(5):
        sofar = None
        for first in range(0, deep, step):
            term = gram(first, min(step, deep - first), dy)
            sofar = term if sofar is None else sofar + term
        sums.append(sofar)

    zero0 = [None, None, sums[0]]
    zero0[1] = sums[0] - line_gram(total - 1, 0)
    zero0[0] = zero0[1] - line_gram(total - 2, 0)
    zero0.append(sums[0] - line_gram(0, 0))
    zero0.append(zero0[3] - line_gram(1, 0))
    one = [sums[1] - line_gram(total - 2, 1), sums[1], sums[1], sums[1] - line_gram(0, 1)]

    row_i = lax.broadcasted_iota(jnp.int32, (size, size), 0)
    col_i = lax.broadcasted_iota(jnp.int32, (size, size), 1)
    per_frame = size // (2 * frames)
    row_frame = row_i // per_frame % frames
    col_frame = col_i // per_frame % frames
    col_part = col_i // (size // 2)
    weight = jnp.zeros((size, size), jnp.float32)
    for s in range(frames):
        reach = sum(1 for t in range(frames) if abs(s - t) <= 2)
        weight = jnp.where(row_frame == s, float(reach), weight)
    diagonal = zero0[0] + zero0[1] + zero0[2] + zero0[3] + zero0[4]
    diagonal = jnp.where(row_i == col_i, diagonal * weight, 0.0)
    trace = jnp.sum(jnp.sum(diagonal, axis=0, keepdims=True), axis=1, keepdims=True)
    scale = trace / (125 * coils) + 1e-06

    table = couplings(frames)
    half = size // 2

    def lane_roll(x, by):
        by = by % size
        return x if by == 0 else jnp.concatenate([x[:, size - by :], x[:, : size - by]], axis=1)

    def mixed(raw):
        swapped = lane_roll(raw, half)
        sign = jnp.where(col_part[:half] == 0, 1.0, -1.0)
        whole = jnp.concatenate(
            [raw[:half] + sign * swapped[half:], raw[half:] - sign * swapped[:half]], axis=0
        )
        result = jnp.zeros_like(whole)
        for d in range(1 - frames, frames):
            terms = {k: v for k, v in table.items() if k[2] == d}
            if not terms:
                continue
            by = d * per_frame
            moved = lane_roll(whole, -by)
            if by % size:
                moved = jnp.concatenate([moved[by % size :], moved[: by % size]], axis=0)
            factor = jnp.zeros_like(whole)
            for (s, s2, _), v in terms.items():
                factor = jnp.where((row_frame == s) & (col_frame == s2), float(v), factor)
            result = result + factor * moved
        return result

    def put(row, col, x):
        hi, lo = halves(x)
        m_hi[col, pl.ds(row * size, size), :] = hi
        m_lo[col, pl.ds(row * size, size), :] = lo

    for b in range(5):
        put(b, b, mixed(zero0[b]))
    kept = None
    for b in range(4):
        if b != 2:
            kept = mixed(one[b])
            turned = kept.T
        put(b + 1, b, kept)
        put(b, b + 1, turned)
    for dy in range(2, 5):
        kept = mixed(sums[dy])
        turned = kept.T
        for b in range(5 - dy):
            put(b + dy, b, kept)
            put(b, b + dy, turned)

    wide = near * LANES
    cell = lax.broadcasted_iota(jnp.int32, (1, wide), 1)
    cell_slot = cell % LANES // stride
    line = cell // LANES + near * cell_slot
    usable = (cell % LANES % stride < readout) & (cell_slot < fit) & (line < rows + 4)
    line = line + me * rows - 2
    usable = usable & (line >= 0) & (line < total)
    gathers = {}
    for b2 in range(5):
        at = pl.ds(b2 * size, size)
        piece = jnp.zeros((size, wide), jnp.float32)
        for b in range(5):
            cols = pl.ds(b * LANES, wide)
            piece = piece + (
                dot_nn(m_hi[b, at, :], p_hi[:, cols])
                + dot_nn(m_hi[b, at, :], p_lo[:, cols])
                + dot_nn(m_lo[b, at, :], p_hi[:, cols])
            )
        piece = jnp.where(usable, piece, 0.0)
        for e in range(5):
            part = jnp.concatenate(
                [
                    piece[(g * 5 + e) * coils : (g * 5 + e + 1) * coils]
                    for g in range(2 * frames)
                ],
                axis=0,
            )
            for j in range(rows):
                line = j - b2 + 4
                k, g = line % near, line // near
                term = jnp.where(slot == g, part[:, k * LANES : (k + 1) * LANES], 0.0)
                key = (e, j - g)
                gathers[key] = gathers[key] + term if key in gathers else term
    folded = jnp.zeros((channels, LANES), jnp.float32)
    for (e, moves), term in gathers.items():
        by = (moves * stride + e - 2) % LANES
        folded = folded + (pltpu.roll(term, by, 1) if by else term)
    out_ref[...] = folded / (125.0 * scale)


def local(estimate, measured, sampled_lines):
    _, coils, frames, rows, readout = estimate.shape
    n = lax.axis_size("slab")
    place = lax.axis_index("slab")
    stride = readout + 4
    channels = 2 * frames * coils
    size = 5 * channels
    cells = jnp.transpose(estimate, (0, 2, 1, 3, 4)).reshape(channels, rows, readout)
    cells = jnp.pad(cells, ((0, 0), (0, 0), (2, 2))).reshape(channels, rows * stride)
    block = jnp.pad(cells, ((0, 0), (0, LANES - rows * stride)))
    fit = LANES // stride
    deep = -(-n * rows // fit) * LANES
    near = -(-(rows + 4) // fit) * LANES
    bf16 = jnp.bfloat16
    folded = pl.pallas_call(
        functools.partial(whole_kernel, n, (frames, coils, rows, readout)),
        out_shape=jax.ShapeDtypeStruct((channels, LANES), jnp.float32),
        in_specs=[pl.BlockSpec(memory_space=pltpu.VMEM)],
        out_specs=pl.BlockSpec(memory_space=pltpu.VMEM),
        scratch_shapes=[
            pltpu.VMEM((n, channels, LANES), jnp.float32),
            pltpu.SemaphoreType.DMA((n,)),
            pltpu.SemaphoreType.DMA((n,)),
            pltpu.SemaphoreType.DMA,
            pltpu.VMEM((size, deep + 4 * LANES), bf16),
            pltpu.VMEM((size, deep + 4 * LANES), bf16),
            pltpu.VMEM((size, deep), bf16),
            pltpu.VMEM((size, deep), bf16),
            pltpu.VMEM((size, near + 4 * LANES), bf16),
            pltpu.VMEM((size, near + 4 * LANES), bf16),
            pltpu.VMEM((5, 5 * size, size), bf16),
            pltpu.VMEM((5, 5 * size, size), bf16),
        ],
        compiler_params=pltpu.CompilerParams(
            vmem_limit_bytes=48 * 1024 * 1024, collective_id=0, has_side_effects=True
        ),
    )(block)
    folded = folded[:, : rows * stride].reshape(2, frames, coils, rows, stride)[..., :readout]
    folded = jnp.transpose(folded, (0, 2, 1, 3, 4))
    line_index = place * rows + jnp.arange(rows, dtype=jnp.int32)
    hit = jnp.any(sampled_lines[:, :, None] == line_index[None, None, :], axis=1)
    return jnp.where(hit[None, None, :, :, None], measured, folded)


def solution(mesh):
    placed = (
        P(None, None, "grp", "slab", None),
        P(None, None, "grp", "slab", None),
        P("grp", None),
    )
    return jax.shard_map(
        local,
        mesh=mesh,
        in_specs=placed,
        out_specs=P(None, None, "grp", "slab", None),
        check_vma=False,
    )
```

```python
import functools

import jax
import jax.numpy as jnp
from jax import lax
from jax.experimental import pallas as pl
from jax.experimental.pallas import tpu as pltpu
from jax.sharding import PartitionSpec as P

LANES = 128


def gather_kernel(n, x_ref, out_ref, send_sem, recv_sem, own_sem):
    me = lax.axis_index("slab")

    def greet(k, carry):
        pl.semaphore_signal(
            pltpu.get_barrier_semaphore(), inc=1, device_id={"slab": lax.rem(me + k, n)}
        )
        return carry

    lax.fori_loop(1, n, greet, 0)
    own = pltpu.make_async_copy(x_ref, out_ref.at[me], own_sem)
    own.start()
    pl.semaphore_wait(pltpu.get_barrier_semaphore(), n - 1)

    def copy(k, place):
        return pltpu.make_async_remote_copy(
            src_ref=x_ref,
            dst_ref=out_ref.at[place],
            send_sem=send_sem.at[k - 1],
            recv_sem=recv_sem.at[k - 1],
            device_id={"slab": lax.rem(me + k, n)},
        )

    def send(k, carry):
        copy(k, me).start()
        return carry

    def receive(k, carry):
        copy(k, lax.rem(me + n - k, n)).wait_recv()
        return carry

    def finish(k, carry):
        copy(k, me).wait_send()
        return carry

    lax.fori_loop(1, n, send, 0)
    own.wait()
    lax.fori_loop(1, n, receive, 0)
    lax.fori_loop(1, n, finish, 0)


def whole_kernel(n, sizes, x_ref, out_ref, all_ref, send_sem, recv_sem, own_sem, *scratch):
    gather_kernel(n, x_ref, all_ref, send_sem, recv_sem, own_sem)
    filter_kernel(n, *sizes, all_ref, out_ref, *scratch)


def couplings(frames):
    table = {}
    for s in range(frames):
        for s2 in range(frames):
            for d in range(1 - frames, frames):
                if 0 <= s + d < frames and 0 <= s2 + d < frames:
                    n = sum(
                        1
                        for t in range(frames)
                        if 0 <= t + d < frames and abs(s - t) <= 2 and abs(s2 - t) <= 2
                    )
                    if n:
                        table[s, s2, d] = n
    return table


def halves(x):
    hi = x.astype(jnp.bfloat16)
    return hi, (x - hi.astype(jnp.float32)).astype(jnp.bfloat16)


def dot_nt(a, b):
    return lax.dot_general(a, b, (((1,), (1,)), ((), ())), preferred_element_type=jnp.float32)


def dot_nn(a, b):
    return lax.dot_general(a, b, (((1,), (0,)), ((), ())), preferred_element_type=jnp.float32)


def filter_kernel(n, frames, coils, rows, readout, all_ref, out_ref, *scratch):
    q_hi, q_lo, l_hi, l_lo, p_hi, p_lo, m_hi, m_lo = scratch
    me = lax.axis_index("slab")
    stride = readout + 4
    fit = LANES // stride
    channels = 2 * frames * coils
    size = 5 * channels
    total = n * rows
    deep = -(-total // fit)
    near = -(-(rows + 4) // fit)
    lane = lax.broadcasted_iota(jnp.int32, (1, LANES), 1)
    slot = lane // stride
    valid = (lane % stride < readout) & (slot < fit)

    def tile(lines):
        result = jnp.zeros((channels, LANES), jnp.float32)
        for g, source in enumerate(lines):
            if source is not None:
                block, j = source
                by = (g - j) * stride % LANES
                moved = pltpu.roll(block, by, 1) if by else block
                result = jnp.where(slot == g, moved, result)
        return result

    def spread(cells):
        moved = [pltpu.roll(cells, LANES - e, 1) if e else cells for e in range(5)]
        return jnp.concatenate(
            [
                moved[e][g * coils : (g + 1) * coils]
                for g in range(2 * frames)
                for e in range(5)
            ],
            axis=0,
        )

    for k in range(deep + 4):
        lines = []
        for g in range(fit):
            line = k + deep * g
            lines.append((all_ref[line // rows], line % rows) if line < total else None)
        hi, lo = halves(spread(tile(lines)))
        at = pl.ds(k * LANES, LANES)
        q_hi[:, at] = hi
        q_lo[:, at] = lo
        if k < deep:
            l_hi[:, at] = jnp.where(valid, hi, jnp.zeros_like(hi))
            l_lo[:, at] = jnp.where(valid, lo, jnp.zeros_like(lo))

    for k in range(near + 4):
        lines = []
        for g in range(fit):
            line = k + near * g - 4
            other = me + line // rows
            block = all_ref[jnp.clip(other, 0, n - 1)]
            lines.append((jnp.where((other >= 0) & (other < n), block, 0.0), line % rows))
        hi, lo = halves(spread(tile(lines)))
        p_hi[:, pl.ds(k * LANES, LANES)] = hi
        p_lo[:, pl.ds(k * LANES, LANES)] = lo

    def gram(first, count):
        left = pl.ds(first * LANES, count * LANES)
        right = [pl.ds((first + dy) * LANES, count * LANES) for dy in range(5)]
        hi = jnp.concatenate([q_hi[:, at] for at in right], axis=0)
        lo = jnp.concatenate([q_lo[:, at] for at in right], axis=0)
        return dot_nt(hi, l_hi[:, left]) + dot_nt(hi, l_lo[:, left]) + dot_nt(lo, l_hi[:, left])

    def line_gram(line, dy):
        left = pl.ds(line % deep * LANES, LANES)
        right = pl.ds((line % deep + dy) * LANES, LANES)
        pick = slot == line // deep
        hi = jnp.where(pick, l_hi[:, left], 0)
        lo = jnp.where(pick, l_lo[:, left], 0)
        return dot_nt(q_hi[:, right], hi) + dot_nt(q_hi[:, right], lo) + dot_nt(q_lo[:, right], hi)

    step = 16
    sofar = None
    for first in range(0, deep, step):
        term = gram(first, min(step, deep - first))
        sofar = term if sofar is None else sofar + term
    sums = [sofar[dy * size : (dy + 1) * size] for dy in range(5)]

    zero0 = [None, None, sums[0]]
    zero0[1] = sums[0] - line_gram(total - 1, 0)
    zero0[0] = zero0[1] - line_gram(total - 2, 0)
    zero0.append(sums[0] - line_gram(0, 0))
    zero0.append(zero0[3] - line_gram(1, 0))
    one = [sums[1] - line_gram(total - 2, 1), sums[1], sums[1], sums[1] - line_gram(0, 1)]

    row_i = lax.broadcasted_iota(jnp.int32, (size, size), 0)
    col_i = lax.broadcasted_iota(jnp.int32, (size, size), 1)
    per_frame = size // (2 * frames)
    row_frame = row_i // per_frame % frames
    col_frame = col_i // per_frame % frames
    col_part = col_i // (size // 2)
    weight = jnp.zeros((size, size), jnp.float32)
    for s in range(frames):
        reach = sum(1 for t in range(frames) if abs(s - t) <= 2)
        weight = jnp.where(row_frame == s, float(reach), weight)
    diagonal = zero0[0] + zero0[1] + zero0[2] + zero0[3] + zero0[4]
    diagonal = jnp.where(row_i == col_i, diagonal * weight, 0.0)
    trace = jnp.sum(jnp.sum(diagonal, axis=0, keepdims=True), axis=1, keepdims=True)
    scale = trace / (125 * coils) + 1e-06

    table = couplings(frames)
    half = size // 2

    def lane_roll(x, by):
        by = by % size
        return x if by == 0 else jnp.concatenate([x[:, size - by :], x[:, : size - by]], axis=1)

    def mixed(raw):
        swapped = lane_roll(raw, half)
        sign = jnp.where(col_part[:half] == 0, 1.0, -1.0)
        whole = jnp.concatenate(
            [raw[:half] + sign * swapped[half:], raw[half:] - sign * swapped[:half]], axis=0
        )
        result = jnp.zeros_like(whole)
        for d in range(1 - frames, frames):
            terms = {k: v for k, v in table.items() if k[2] == d}
            if not terms:
                continue
            by = d * per_frame
            moved = lane_roll(whole, -by)
            if by % size:
                moved = jnp.concatenate([moved[by % size :], moved[: by % size]], axis=0)
            factor = jnp.zeros_like(whole)
            for (s, s2, _), v in terms.items():
                factor = jnp.where((row_frame == s) & (col_frame == s2), float(v), factor)
            result = result + factor * moved
        return result

    def put(row, col, x):
        hi, lo = halves(x)
        m_hi[col, pl.ds(row * size, size), :] = hi
        m_lo[col, pl.ds(row * size, size), :] = lo

    for b in range(5):
        put(b, b, mixed(zero0[b]))
    kept = None
    for b in range(4):
        if b != 2:
            kept = mixed(one[b])
            turned = kept.T
        put(b + 1, b, kept)
        put(b, b + 1, turned)
    for dy in range(2, 5):
        kept = mixed(sums[dy])
        turned = kept.T
        for b in range(5 - dy):
            put(b + dy, b, kept)
            put(b, b + dy, turned)

    wide = near * LANES
    cell = lax.broadcasted_iota(jnp.int32, (1, wide), 1)
    cell_slot = cell % LANES // stride
    line = cell // LANES + near * cell_slot
    usable = (cell % LANES % stride < readout) & (cell_slot < fit) & (line < rows + 4)
    line = line + me * rows - 2
    usable = usable & (line >= 0) & (line < total)
    gathers = {}
    for b2 in range(5):
        at = pl.ds(b2 * size, size)
        piece = jnp.zeros((size, wide), jnp.float32)
        for b in range(5):
            cols = pl.ds(b * LANES, wide)
            piece = piece + (
                dot_nn(m_hi[b, at, :], p_hi[:, cols])
                + dot_nn(m_hi[b, at, :], p_lo[:, cols])
                + dot_nn(m_lo[b, at, :], p_hi[:, cols])
            )
        piece = jnp.where(usable, piece, 0.0)
        for e in range(5):
            part = jnp.concatenate(
                [
                    piece[(g * 5 + e) * coils : (g * 5 + e + 1) * coils]
                    for g in range(2 * frames)
                ],
                axis=0,
            )
            for j in range(rows):
                line = j - b2 + 4
                k, g = line % near, line // near
                term = jnp.where(slot == g, part[:, k * LANES : (k + 1) * LANES], 0.0)
                key = (e, j - g)
                gathers[key] = gathers[key] + term if key in gathers else term
    folded = jnp.zeros((channels, LANES), jnp.float32)
    for (e, moves), term in gathers.items():
        by = (moves * stride + e - 2) % LANES
        folded = folded + (pltpu.roll(term, by, 1) if by else term)
    out_ref[...] = folded / (125.0 * scale)


def local(estimate, measured, sampled_lines):
    _, coils, frames, rows, readout = estimate.shape
    n = lax.axis_size("slab")
    place = lax.axis_index("slab")
    stride = readout + 4
    channels = 2 * frames * coils
    size = 5 * channels
    cells = jnp.transpose(estimate, (0, 2, 1, 3, 4)).reshape(channels, rows, readout)
    cells = jnp.pad(cells, ((0, 0), (0, 0), (2, 2))).reshape(channels, rows * stride)
    block = jnp.pad(cells, ((0, 0), (0, LANES - rows * stride)))
    fit = LANES // stride
    deep = -(-n * rows // fit) * LANES
    near = -(-(rows + 4) // fit) * LANES
    bf16 = jnp.bfloat16
    folded = pl.pallas_call(
        functools.partial(whole_kernel, n, (frames, coils, rows, readout)),
        out_shape=jax.ShapeDtypeStruct((channels, LANES), jnp.float32),
        in_specs=[pl.BlockSpec(memory_space=pltpu.VMEM)],
        out_specs=pl.BlockSpec(memory_space=pltpu.VMEM),
        scratch_shapes=[
            pltpu.VMEM((n, channels, LANES), jnp.float32),
            pltpu.SemaphoreType.DMA((n,)),
            pltpu.SemaphoreType.DMA((n,)),
            pltpu.SemaphoreType.DMA,
            pltpu.VMEM((size, deep + 4 * LANES), bf16),
            pltpu.VMEM((size, deep + 4 * LANES), bf16),
            pltpu.VMEM((size, deep), bf16),
            pltpu.VMEM((size, deep), bf16),
            pltpu.VMEM((size, near + 4 * LANES), bf16),
            pltpu.VMEM((size, near + 4 * LANES), bf16),
            pltpu.VMEM((5, 5 * size, size), bf16),
            pltpu.VMEM((5, 5 * size, size), bf16),
        ],
        compiler_params=pltpu.CompilerParams(
            vmem_limit_bytes=48 * 1024 * 1024, collective_id=0, has_side_effects=True
        ),
    )(block)
    folded = folded[:, : rows * stride].reshape(2, frames, coils, rows, stride)[..., :readout]
    folded = jnp.transpose(folded, (0, 2, 1, 3, 4))
    line_index = place * rows + jnp.arange(rows, dtype=jnp.int32)
    hit = jnp.any(sampled_lines[:, :, None] == line_index[None, None, :], axis=1)
    return jnp.where(hit[None, None, :, :, None], measured, folded)


def solution(mesh):
    placed = (
        P(None, None, "grp", "slab", None),
        P(None, None, "grp", "slab", None),
        P("grp", None),
    )
    return jax.shard_map(
        local,
        mesh=mesh,
        in_specs=placed,
        out_specs=P(None, None, "grp", "slab", None),
        check_vma=False,
    )
```
